32 devices in a mesh: wide: 8 (over z, x), narrow: 4 (over y, core).
Axes of the slice: x: 2, y: 2, z: 4, core: 2. Of those that a mesh axis runs over, the one named last changes fastest.
Arguments:
- tokens: bfloat16 [4096, 2048], P(('wide', 'narrow')), may hold values from -6 to 6
- expert_ids: int32 [4096], P(('wide', 'narrow')), may hold values from 0 to 3, as said below
- route_weights: float32 [4096], P(('wide', 'narrow')), may hold values from 0.2 to 1
- out_grad: bfloat16 [4096, 2048], P(('wide', 'narrow')), may hold values from -0.796875 to 0.796875
- w_gate_up: bfloat16 [32, 2048, 256], P(('wide', 'narrow')), may hold values from -0.125 to 0.125
- w_down: bfloat16 [32, 128, 2048], P(('wide', 'narrow')), may hold values from -0.375 to 0.375
- second_moment: bfloat16 [32, 128, 2048], P(('wide', 'narrow')), may hold values from 0.0049743652 to 0.099609375
Outputs:
- grad_gate_up: bfloat16 [32, 2048, 256], P(('wide', 'narrow'))
- down_update: bfloat16 [32, 128, 2048], P(('wide', 'narrow'))
The draws below stay inside these ranges and needn't reach their ends.
Inputs may be any that keep to these rules, and one draw needn't show every extreme that they name: `expert_ids`: values below 2 name the token's own group's experts, the others the next group's. Within the rows of one device no value appears more than 48 times; in every group of 4 devices along narrow one value appears exactly 48 times on every device of the group.
All inputs are finite; a program needn't handle non-finite values.
Results may differ from the reference program's by a relative error of at most 0.0066.
Values may be sent and summed in bfloat16 or wider, within the bound.
A program may use at most 64 MiB of HBM per device.

```python
import math
import jax
import jax.numpy as jnp
from jax import lax

D = 2048
FF = 256
TOK_DEV = 128
HALF = 128
CAP = 48
TOKENS = 4096
SLABS = 32
N_WIDE = 8
N_NARROW = 4


def draw_expert_ids(key, part):
    groups = N_NARROW
    others = groups - 1
    remaining = TOK_DEV - CAP
    base_count = remaining // others
    extra_count = remaining - base_count * others
    pair_count = others // 2
    spread = max(0, min(base_count, CAP - base_count - 1))

    def one_device(device):
        group_key = jax.random.fold_in(jax.random.fold_in(key, 11), device // groups)
        full_expert = jax.random.randint(group_key, (), 0, groups)
        device_key = jax.random.fold_in(jax.random.fold_in(key, 23), device)
        order_key, shift_key, place_key = jax.random.split(device_key, 3)
        shuffle = jax.random.permutation(order_key, others)
        shifts = jax.random.randint(shift_key, (pair_count,), 0, spread + 1)
        signed = jnp.stack([shifts, -shifts], axis=1).reshape(-1)
        signed = jnp.concatenate([signed, jnp.zeros((others - 2 * pair_count,), jnp.int32)])
        counts = base_count + (jnp.arange(others) < extra_count).astype(jnp.int32) + signed
        owners = (full_expert + 1 + shuffle) % groups
        totals = jnp.zeros((groups,), jnp.int32).at[owners].set(counts).at[full_expert].set(CAP)
        bounds = jnp.cumsum(totals)
        positions = jnp.arange(TOK_DEV)
        labels = jnp.sum((positions[:, None] >= bounds[None, :]).astype(jnp.int32), axis=1)
        return labels[jax.random.permutation(place_key, TOK_DEV)]
    return jax.vmap(one_device)(jnp.arange(TOKENS // TOK_DEV)).reshape(-1).astype(jnp.int32)


def level_of(rng, dims, cuts, smallest, largest):
    def one(dim, blocks):
        steps = jax.random.uniform(jax.random.fold_in(jax.random.fold_in(rng, 6), dim), (blocks,), jnp.float32, smallest / len(cuts), largest / len(cuts))
        return jnp.repeat(jnp.exp(steps), dims[dim] // blocks).reshape((-1,) + (1,) * (len(dims) - dim - 1))

    loudness = one(*cuts[0])
    for cut in cuts[1:]:
        loudness = loudness * one(*cut)
    return loudness


def bell_draw(own_key, dims, width, most, cuts=(), kind=jnp.bfloat16):
    factor_of = level_of(own_key, dims, cuts, -0.22, 0.18) if cuts else 1.0
    drawn = jax.random.normal(own_key, dims, jnp.float32) * width * factor_of
    return jnp.minimum(jnp.maximum(drawn, -most), most).astype(kind)


def setup_inputs(seed: int = 0) -> dict:
    key_list = jax.random.split(jax.random.key(seed), 8)
    return {
        "tokens": bell_draw(key_list[0], (TOKENS, D), 1.0, 6.0, ((0, 32),)),
        "expert_ids": draw_expert_ids(jax.random.fold_in(key_list[7], 71), 0),
        "route_weights": jnp.clip(0.2 + 0.8 * jax.random.uniform(key_list[2], (TOKENS,), jnp.float32) ** level_of(key_list[2], (TOKENS,), ((0, 32),), -0.2, 0.2), 0.2, 1.0),
        "out_grad": bell_draw(key_list[3], (TOKENS, D), 0.1, 0.796875, ((0, 32),)),
        "w_gate_up": bell_draw(key_list[4], (SLABS, D, FF), D ** -0.5, 0.125, ((0, 32),)),
        "w_down": bell_draw(key_list[5], (SLABS, HALF, D), FF ** -0.5, 0.375, ((0, 32),)),
        "second_moment": jnp.clip(jnp.exp(math.log(0.099609375) - 2.9969585 * jax.random.uniform(key_list[6], (SLABS, HALF, D), jnp.float32) ** level_of(key_list[6], (SLABS, HALF, D), ((0, 32),), -0.2, 0.2)), 0.0049743652, 0.099609375).astype(jnp.bfloat16),
    }


second_correction = 1.0 - 0.95 ** 10

def term_grads(rows_x, rows_d, weight_gu, weight_dn):
    width_half = weight_dn.shape[0]
    projected = jnp.dot(rows_x, weight_gu, preferred_element_type=jnp.float32)
    gate_pre = projected[:, :width_half]
    up_pre = projected[:, width_half:]
    logistic = jax.nn.sigmoid(gate_pre)
    swished = gate_pre * logistic
    hidden = (swished * up_pre).astype(jnp.bfloat16)
    down_grad = jnp.dot(hidden.T, rows_d, preferred_element_type=jnp.float32)
    hidden_grad = jnp.dot(rows_d, weight_dn.T, preferred_element_type=jnp.float32)
    gate_grad = hidden_grad * up_pre * logistic * (1.0 + gate_pre * (1.0 - logistic))
    up_grad = hidden_grad * swished
    pre_grads = jnp.concatenate([gate_grad, up_grad], axis=1).astype(jnp.bfloat16)
    proj_grad = jnp.dot(rows_x.T, pre_grads, preferred_element_type=jnp.float32)
    return (proj_grad, down_grad)

def dispatch_rows(rows, labels):
    experts_axis = jnp.arange(N_NARROW, dtype=jnp.int32)
    onehot = (labels[:, None] == experts_axis[None, :]).astype(jnp.int32)
    within = lax.optimization_barrier(jnp.sum((jnp.cumsum(onehot, axis=0) - onehot) * onehot, axis=1))
    target = labels * CAP + within
    columns = jnp.arange(N_NARROW * CAP, dtype=jnp.int32)
    select = (target[:, None] == columns[None, :]).astype(rows.dtype)
    placed = jnp.dot(select.T, rows, preferred_element_type=jnp.float32).astype(rows.dtype)
    return placed.reshape(N_NARROW, CAP, D)

def reference(tokens, expert_ids, route_weights, out_grad, w_gate_up, w_down, second_moment):
    devices = N_WIDE * N_NARROW
    half_groups = N_NARROW // 2
    scaled = (route_weights[:, None] * out_grad.astype(jnp.float32)).astype(jnp.bfloat16)
    labels = expert_ids.reshape(devices, TOK_DEV)
    row_buffers = jax.vmap(dispatch_rows)(tokens.reshape(devices, TOK_DEV, D), labels)
    grad_buffers = jax.vmap(dispatch_rows)(scaled.reshape(devices, TOK_DEV, D), labels)
    row_buffers = row_buffers.reshape(N_WIDE, N_NARROW, N_NARROW, CAP, D)
    grad_buffers = grad_buffers.reshape(N_WIDE, N_NARROW, N_NARROW, CAP, D)

    def per_slab(slab_index):
        wide_index = slab_index // N_NARROW
        narrow_index = slab_index % N_NARROW
        previous = (wide_index + N_WIDE - 1) % N_WIDE
        local_expert = narrow_index // 2
        own_x = row_buffers[wide_index, :, local_expert].reshape(N_NARROW * CAP, D)
        own_d = grad_buffers[wide_index, :, local_expert].reshape(N_NARROW * CAP, D)
        near_x = row_buffers[previous, :, half_groups + local_expert].reshape(N_NARROW * CAP, D)
        near_d = grad_buffers[previous, :, half_groups + local_expert].reshape(N_NARROW * CAP, D)
        weight_gu = w_gate_up[slab_index]
        weight_dn = w_down[slab_index]
        own_proj, own_down = term_grads(own_x, own_d, weight_gu, weight_dn)
        near_proj, near_down = term_grads(near_x, near_d, weight_gu, weight_dn)
        rounded = lax.optimization_barrier((near_proj.astype(jnp.bfloat16), near_down.astype(jnp.bfloat16)))
        total_proj = own_proj + rounded[0].astype(jnp.float32)
        total_down = own_down + rounded[1].astype(jnp.float32)
        second = 0.95 * second_moment[slab_index].astype(jnp.float32) + 0.05 * total_down * total_down
        update = total_down / (jnp.sqrt(second / second_correction) + 1e-08) + 0.1 * weight_dn.astype(jnp.float32)
        return (total_proj.astype(jnp.bfloat16), update.astype(jnp.bfloat16))
    grad_gate_up, down_update = lax.map(per_slab, jnp.arange(devices, dtype=jnp.int32))
    return (grad_gate_up, down_update)
```

```python
import functools

import jax
import jax.numpy as jnp
from jax import lax
from jax.experimental import pallas as pl
from jax.experimental.pallas import tpu as pltpu
from jax.sharding import PartitionSpec as P

second_correction = 1.0 - 0.95**10
bf16 = jnp.bfloat16
f32 = jnp.float32


def mm(a, b, dims):
    return lax.dot_general(a, b, (dims, ((), ())), preferred_element_type=f32)


def kernel(
    groups, wides, cap, slot, chunks,
    ids, rw, tok_hbm, og_hbm, wgu_hbm, wdn_hbm, sm_hbm,
    gout, uout,
    tok, og, wgu, wdn, sm, px, pd, rx, rd, pre, hid, acc_p, acc_d, gstage, ustage,
    in_sem, out_sem, sx, rxs, sd, rds, sc, rcs, fsx, frx, fsd, frd, fsc, frc,
):
    half = groups // 2
    width = tok.shape[1]
    hidden_units = wdn.shape[0]
    wide = lax.axis_index("wide")
    narrow = lax.axis_index("narrow")
    home = narrow // 2
    parity = lax.rem(narrow, 2)
    ahead = lax.rem(wide + 1, wides)
    behind = lax.rem(wide + wides - 1, wides)

    def device(w, n):
        return {"wide": w, "narrow": n}

    def expert_at(j):
        return lax.rem(home + j, half)

    sibling = device(wide, 2 * home + 1 - parity)

    order = [(0, 0), (1, 0)] + [(0, j) for j in range(1, half)] + [(1, j) for j in range(1, half)]
    early = 2 + (half - 1)
    late = half - 1
    remote_early = list(range(1, early))
    late_list = list(range(early, early + late))

    loads = []
    for i, (src, dst) in enumerate(
        ((tok_hbm, tok), (og_hbm, og), (wgu_hbm.at[0], wgu), (wdn_hbm.at[0], wdn), (sm_hbm.at[0], sm))
    ):
        copy = pltpu.make_async_copy(src, dst, in_sem.at[i])
        copy.start()
        loads.append(copy)

    barrier = pltpu.get_barrier_semaphore()
    partners = [sibling]
    for j in range(half):
        if j:
            partners.append(device(wide, 2 * expert_at(j) + parity))
        partners.append(device(ahead, 2 * expert_at(j) + parity))
        partners.append(device(behind, 2 * expert_at(j) + parity))
    for partner in partners:
        pl.semaphore_signal(barrier, inc=1, device_id=partner, device_id_type=pl.DeviceIdType.MESH)

    count = tok.shape[0]
    labels = ids[...]
    pad_groups = max(8, groups)
    onehot = (lax.broadcasted_iota(jnp.int32, (pad_groups, count), 0) == labels).astype(f32)
    before = (
        lax.broadcasted_iota(jnp.int32, (count, count), 0)
        < lax.broadcasted_iota(jnp.int32, (count, count), 1)
    ).astype(f32)
    counted = mm(onehot.astype(bf16), before.astype(bf16), ((1,), (0,)))
    within = jnp.sum(counted * onehot, axis=0, keepdims=True).astype(jnp.int32)
    weights = rw[...]
    slots = lax.broadcasted_iota(jnp.int32, (slot, count), 0)

    def select_of(b):
        kind, j = order[b]
        value = kind * half + expert_at(j)
        return jnp.logical_and(labels == value, slots == within)

    def rows(b, h):
        return pl.ds((2 * b + h) * slot, slot)

    def dest(b):
        kind, j = order[b]
        return device(ahead if kind else wide, 2 * expert_at(j) + parity)

    def remote(src, dst, s, r, dev):
        return pltpu.make_async_remote_copy(
            src_ref=src, dst_ref=dst, send_sem=s, recv_sem=r,
            device_id=dev, device_id_type=pl.DeviceIdType.MESH,
        )

    part = width // chunks

    def send_x(b):
        return remote(px.at[b], rx.at[rows(b, 0)], sx.at[b], rxs.at[b], dest(b))

    def send_d(b):
        return remote(pd.at[b], rd.at[rows(b, 0)], sd.at[b], rds.at[b], dest(b))

    def send_c(b, c):
        cols = pl.ds(c * part, part)
        i = (b - early) * chunks + c
        return remote(
            pd.at[b, :, cols], rd.at[rows(b, 0), cols], sc.at[i], rcs.at[i], dest(b)
        )

    def forward_x(b):
        return remote(rx.at[rows(b, 0)], rx.at[rows(b, 1)], fsx.at[b], frx.at[b], sibling)

    def forward_d(b):
        return remote(rd.at[rows(b, 0)], rd.at[rows(b, 1)], fsd.at[b], frd.at[b], sibling)

    def forward_c(b, c):
        cols = pl.ds(c * part, part)
        i = (b - early) * chunks + c
        return remote(
            rd.at[rows(b, 0), cols], rd.at[rows(b, 1), cols], fsc.at[i], frc.at[i], sibling
        )

    started = []

    def go(copy):
        copy.start()
        started.append(copy)

    def pack_x(b):
        return mm(select_of(b).astype(f32).astype(bf16), tok[...], ((1,), (0,))).astype(bf16)

    def pack_d(b):
        select = select_of(b)
        weight = jnp.sum(jnp.where(select, weights, 0.0), axis=1, keepdims=True)
        placed = mm(select.astype(f32).astype(bf16), og[...], ((1,), (0,)))
        return (weight * placed).astype(bf16)

    loads[0].wait()
    for b in remote_early:
        px[b] = pack_x(b)
    pl.semaphore_wait(barrier, len(partners))
    for b in remote_early:
        go(send_x(b))
    loads[1].wait()
    for b in remote_early:
        pd[b] = pack_d(b)
    for b in late_list:
        px[b] = pack_x(b)
    for b in remote_early:
        go(send_d(b))
    for b in late_list:
        go(send_x(b))
    for b in late_list:
        pd[b] = pack_d(b)
    rx[rows(0, 0), :] = pack_x(0)
    for b in late_list:
        for c in range(chunks):
            go(send_c(b, c))
    rd[rows(0, 0), :] = pack_d(0)
    go(forward_x(0))
    go(forward_d(0))
    loads[2].wait()
    loads[3].wait()

    def project(r):
        projected = mm(rx[r, :], wgu[...], ((1,), (0,)))
        gate_pre = projected[:, :hidden_units]
        up_pre = projected[:, hidden_units:]
        logistic = jax.nn.sigmoid(gate_pre)
        swished = gate_pre * logistic
        hid[r, :] = (swished * up_pre).astype(bf16)
        return up_pre * logistic * (1.0 + gate_pre * (1.0 - logistic)), swished

    def finish(r, hidden_grad, factors):
        pre[r, :] = jnp.concatenate(
            [hidden_grad * factors[0], hidden_grad * factors[1]], axis=1
        ).astype(bf16)

    for b in remote_early:
        send_x(b).wait_recv()
        go(forward_x(b))
    for b in remote_early:
        send_d(b).wait_recv()
        go(forward_d(b))
    for b in range(early):
        forward_x(b).wait_recv()
        forward_d(b).wait_recv()
    first = pl.ds(0, early * 2 * slot)
    finish(first, mm(rd[first, :], wdn[...], ((1,), (1,))), project(first))
    for i in range(width // 256):
        cols = pl.ds(i * 256, 256)
        acc_p[cols, :] = mm(rx[first, cols], pre[first, :], ((0,), (0,)))
        acc_d[:, cols] = mm(hid[first, :], rd[first, cols], ((0,), (0,)))

    for b in late_list:
        send_x(b).wait_recv()
        go(forward_x(b))
    for b in late_list:
        forward_x(b).wait_recv()
    last = pl.ds(early * 2 * slot, late * 2 * slot)
    factors = project(last)
    loads[4].wait()
    hidden_grad = jnp.zeros((late * 2 * slot, hidden_units), f32)
    outs = []

    def relay(c):
        for b in late_list:
            send_c(b, c).wait_recv()
            go(forward_c(b, c))

    relay(0)
    for c in range(chunks):
        if c + 1 < chunks:
            relay(c + 1)
        for b in late_list:
            forward_c(b, c).wait_recv()
        cols = pl.ds(c * part, part)
        hidden_grad = hidden_grad + mm(rd[last, cols], wdn[:, cols], ((1,), (1,)))
        if c == chunks - 1:
            finish(last, hidden_grad, factors)
            for i in range(width // 256):
                r = pl.ds(i * 256, 256)
                gstage[r, :] = (
                    acc_p[r, :] + mm(rx[last, r], pre[last, :], ((0,), (0,)))
                ).astype(bf16)
                copy = pltpu.make_async_copy(gstage.at[r], gout.at[0, r], out_sem.at[chunks + i])
                copy.start()
                outs.append(copy)
        total = acc_d[:, cols] + mm(hid[last, :], rd[last, cols], ((0,), (0,)))
        second = 0.95 * sm[:, cols].astype(f32) + 0.05 * total * total
        update = total / (jnp.sqrt(second / second_correction) + 1e-08)
        ustage[:, cols] = (update + 0.1 * wdn[:, cols].astype(f32)).astype(bf16)
        copy = pltpu.make_async_copy(ustage.at[:, cols], uout.at[0, :, cols], out_sem.at[c])
        copy.start()
        outs.append(copy)

    for copy in started:
        copy.wait_send()
    for copy in outs:
        copy.wait()


def body(tokens, expert_ids, route_weights, out_grad, w_gate_up, w_down, second_moment):
    groups = lax.axis_size("narrow")
    wides = lax.axis_size("wide")
    count, width = tokens.shape
    cap = 3 * count // (2 * groups)
    slot = -(-cap // 16) * 16
    chunks = 4
    columns = w_gate_up.shape[2]
    units = w_down.shape[1]
    all_rows = groups * 2 * slot
    late = groups // 2 - 1
    dma = pltpu.SemaphoreType.DMA
    any_spec = pl.BlockSpec(memory_space=pl.ANY)
    vmem_spec = pl.BlockSpec(memory_space=pltpu.VMEM)
    return pl.pallas_call(
        functools.partial(kernel, groups, wides, cap, slot, chunks),
        out_shape=(
            jax.ShapeDtypeStruct((1, width, columns), bf16),
            jax.ShapeDtypeStruct((1, units, width), bf16),
        ),
        in_specs=[vmem_spec, vmem_spec] + [any_spec] * 5,
        out_specs=(any_spec, any_spec),
        scratch_shapes=[
            pltpu.VMEM((count, width), bf16),
            pltpu.VMEM((count, width), bf16),
            pltpu.VMEM((width, columns), bf16),
            pltpu.VMEM((units, width), bf16),
            pltpu.VMEM((units, width), bf16),
            pltpu.VMEM((groups, slot, width), bf16),
            pltpu.VMEM((groups, slot, width), bf16),
            pltpu.VMEM((all_rows, width), bf16),
            pltpu.VMEM((all_rows, width), bf16),
            pltpu.VMEM((all_rows, columns), bf16),
            pltpu.VMEM((all_rows, units), bf16),
            pltpu.VMEM((width, columns), f32),
            pltpu.VMEM((units, width), f32),
            pltpu.VMEM((width, columns), bf16),
            pltpu.VMEM((units, width), bf16),
            dma((5,)),
            dma((chunks + width // 256,)),
            dma((groups,)), dma((groups,)), dma((groups,)), dma((groups,)),
            dma((late * chunks,)), dma((late * chunks,)),
            dma((groups,)), dma((groups,)), dma((groups,)), dma((groups,)),
            dma((late * chunks,)), dma((late * chunks,)),
        ],
        compiler_params=pltpu.CompilerParams(collective_id=0, has_side_effects=True),
    )(
        expert_ids.reshape(1, count), route_weights.reshape(1, count),
        tokens, out_grad, w_gate_up, w_down, second_moment,
    )


def solution(mesh):
    placed = (
        P(("wide", "narrow"), None),
        P(("wide", "narrow")),
        P(("wide", "narrow")),
        P(("wide", "narrow"), None),
        P(("wide", "narrow"), None, None),
        P(("wide", "narrow"), None, None),
        P(("wide", "narrow"), None, None),
    )
    return jax.shard_map(
        body,
        mesh=mesh,
        in_specs=placed,
        out_specs=(P(("wide", "narrow"), None, None), P(("wide", "narrow"), None, None)),
        check_vma=False,
    )
```

```python
import functools

import jax
import jax.numpy as jnp
from jax import lax
from jax.experimental import pallas as pl
from jax.experimental.pallas import tpu as pltpu
from jax.sharding import PartitionSpec as P

second_correction = 1.0 - 0.95**10
bf16 = jnp.bfloat16
f32 = jnp.float32
LIMIT = 32 * 1024 * 1024


def mm(a, b, dims):
    return lax.dot_general(a, b, (dims, ((), ())), preferred_element_type=f32)


def kernel(
    groups, wides, cap, slot, chunks,
    ids, rw, tok_hbm, og_hbm, wgu_hbm, wdn_hbm, sm_hbm,
    acc_p, rows_last, pre_last, ustage,
    tok, og, wgu, wdn, sm, px, pd, rx, rd, pre, hid, acc_d,
    in_sem, sx, rxs, sd, rds, sc, rcs, fsx, frx, fsd, frd, fsc, frc,
):
    half = groups // 2
    width = tok.shape[1]
    hidden_units = wdn.shape[0]
    wide = lax.axis_index("wide")
    narrow = lax.axis_index("narrow")
    home = narrow // 2
    parity = lax.rem(narrow, 2)
    ahead = lax.rem(wide + 1, wides)
    behind = lax.rem(wide + wides - 1, wides)

    def device(w, n):
        return {"wide": w, "narrow": n}

    def expert_at(j):
        return lax.rem(home + j, half)

    sibling = device(wide, 2 * home + 1 - parity)

    order = [(0, 0), (1, 0)] + [(0, j) for j in range(1, half)] + [(1, j) for j in range(1, half)]
    early = 2 + (half - 1)
    late = half - 1
    remote_early = list(range(1, early))
    late_list = list(range(early, early + late))

    loads = []
    for i, (src, dst) in enumerate(
        ((tok_hbm, tok), (og_hbm, og), (wgu_hbm.at[0], wgu), (wdn_hbm.at[0], wdn), (sm_hbm.at[0], sm))
    ):
        copy = pltpu.make_async_copy(src, dst, in_sem.at[i])
        copy.start()
        loads.append(copy)

    barrier = pltpu.get_barrier_semaphore()
    partners = [device(behind, 2 * expert_at(j) + parity) for j in range(half)]
    partners += [device(wide, 2 * expert_at(j) + parity) for j in range(1, half)]
    partners.append(sibling)
    for partner in partners:
        pl.semaphore_signal(barrier, inc=1, device_id=partner, device_id_type=pl.DeviceIdType.MESH)

    count = tok.shape[0]
    labels = ids[...]
    pad_groups = max(8, groups)
    onehot = (lax.broadcasted_iota(jnp.int32, (pad_groups, count), 0) == labels).astype(f32)
    before = (
        lax.broadcasted_iota(jnp.int32, (count, count), 0)
        < lax.broadcasted_iota(jnp.int32, (count, count), 1)
    ).astype(f32)
    counted = mm(onehot.astype(bf16), before.astype(bf16), ((1,), (0,)))
    within = jnp.sum(counted * onehot, axis=0, keepdims=True).astype(jnp.int32)
    weights = rw[...]
    slots = lax.broadcasted_iota(jnp.int32, (slot, count), 0)

    def select_of(b):
        kind, j = order[b]
        value = kind * half + expert_at(j)
        return jnp.logical_and(labels == value, slots == within)

    def rows(b, h):
        return pl.ds((2 * b + h) * slot, slot)

    def dest(b):
        kind, j = order[b]
        return device(ahead if kind else wide, 2 * expert_at(j) + parity)

    def remote(src, dst, s, r, dev):
        return pltpu.make_async_remote_copy(
            src_ref=src, dst_ref=dst, send_sem=s, recv_sem=r,
            device_id=dev, device_id_type=pl.DeviceIdType.MESH,
        )

    part = width // chunks

    def send_x(b):
        return remote(px.at[b], rx.at[rows(b, 0)], sx.at[b], rxs.at[b], dest(b))

    def send_d(b):
        return remote(pd.at[b], rd.at[rows(b, 0)], sd.at[b], rds.at[b], dest(b))

    def send_c(b, c):
        cols = pl.ds(c * part, part)
        i = (b - early) * chunks + c
        return remote(
            pd.at[b, :, cols], rd.at[rows(b, 0), cols], sc.at[i], rcs.at[i], dest(b)
        )

    def forward_x(b):
        return remote(rx.at[rows(b, 0)], rx.at[rows(b, 1)], fsx.at[b], frx.at[b], sibling)

    def forward_d(b):
        return remote(rd.at[rows(b, 0)], rd.at[rows(b, 1)], fsd.at[b], frd.at[b], sibling)

    def forward_c(b, c):
        cols = pl.ds(c * part, part)
        i = (b - early) * chunks + c
        return remote(
            rd.at[rows(b, 0), cols], rd.at[rows(b, 1), cols], fsc.at[i], frc.at[i], sibling
        )

    started = []

    def go(copy):
        copy.start()
        started.append(copy)

    def pack_x(b):
        return mm(select_of(b).astype(f32).astype(bf16), tok[...], ((1,), (0,))).astype(bf16)

    def pack_d(b):
        select = select_of(b)
        weight = jnp.sum(jnp.where(select, weights, 0.0), axis=1, keepdims=True)
        placed = mm(select.astype(f32).astype(bf16), og[...], ((1,), (0,)))
        return (weight * placed).astype(bf16)

    loads[0].wait()
    for b in remote_early:
        px[b] = pack_x(b)
    pl.semaphore_wait(barrier, len(partners))
    for b in remote_early:
        go(send_x(b))
    loads[1].wait()
    for b in remote_early:
        pd[b] = pack_d(b)
    for b in late_list:
        px[b] = pack_x(b)
    for b in remote_early:
        go(send_d(b))
    for b in late_list:
        go(send_x(b))
    for b in late_list:
        pd[b] = pack_d(b)
    rx[rows(0, 0), :] = pack_x(0)
    for b in late_list:
        for c in range(chunks):
            go(send_c(b, c))
    rd[rows(0, 0), :] = pack_d(0)
    go(forward_x(0))
    go(forward_d(0))
    loads[2].wait()
    loads[3].wait()

    def project(r):
        projected = mm(rx[r, :], wgu[...], ((1,), (0,)))
        gate_pre = projected[:, :hidden_units]
        up_pre = projected[:, hidden_units:]
        logistic = jax.nn.sigmoid(gate_pre)
        swished = gate_pre * logistic
        hid[r, :] = (swished * up_pre).astype(bf16)
        return up_pre * logistic * (1.0 + gate_pre * (1.0 - logistic)), swished

    def finish(target, r, hidden_grad, factors):
        target[r, :] = jnp.concatenate(
            [hidden_grad * factors[0], hidden_grad * factors[1]], axis=1
        ).astype(bf16)

    for b in remote_early:
        send_x(b).wait_recv()
        go(forward_x(b))
    for b in remote_early:
        send_d(b).wait_recv()
        go(forward_d(b))
    for b in range(early):
        forward_x(b).wait_recv()
        forward_d(b).wait_recv()
    first = pl.ds(0, early * 2 * slot)
    finish(pre, first, mm(rd[first, :], wdn[...], ((1,), (1,))), project(first))
    for i in range(width // 256):
        cols = pl.ds(i * 256, 256)
        acc_p[cols, :] = mm(rx[first, cols], pre[first, :], ((0,), (0,)))
        acc_d[:, cols] = mm(hid[first, :], rd[first, cols], ((0,), (0,)))

    for b in late_list:
        send_x(b).wait_recv()
        go(forward_x(b))
    for b in late_list:
        forward_x(b).wait_recv()
    last = pl.ds(early * 2 * slot, late * 2 * slot)
    factors = project(last)
    rows_last[...] = rx[last, :]
    loads[4].wait()
    hidden_grad = jnp.zeros((late * 2 * slot, hidden_units), f32)

    def relay(c):
        for b in late_list:
            send_c(b, c).wait_recv()
            go(forward_c(b, c))

    relay(0)
    for c in range(chunks):
        if c + 1 < chunks:
            relay(c + 1)
        for b in late_list:
            forward_c(b, c).wait_recv()
        cols = pl.ds(c * part, part)
        hidden_grad = hidden_grad + mm(rd[last, cols], wdn[:, cols], ((1,), (1,)))
        total = acc_d[:, cols] + mm(hid[last, :], rd[last, cols], ((0,), (0,)))
        second = 0.95 * sm[:, cols].astype(f32) + 0.05 * total * total
        update = total / (jnp.sqrt(second / second_correction) + 1e-08)
        ustage[:, cols] = (update + 0.1 * wdn[:, cols].astype(f32)).astype(bf16)

    finish(pre_last, slice(None), hidden_grad, factors)
    for copy in started:
        copy.wait_send()


def final_kernel(acc_p, rows_last, pre_last, update, gout, uout, gstage, out_sem):
    tiles = acc_p.shape[0] // 256
    outs = [pltpu.make_async_copy(update, uout.at[0], out_sem.at[tiles])]
    outs[0].start()
    for i in range(tiles):
        r = pl.ds(i * 256, 256)
        gstage[r, :] = (acc_p[r, :] + mm(rows_last[:, r], pre_last[...], ((0,), (0,)))).astype(bf16)
        copy = pltpu.make_async_copy(gstage.at[r], gout.at[0, r], out_sem.at[i])
        copy.start()
        outs.append(copy)
    for copy in outs:
        copy.wait()


def body(tokens, expert_ids, route_weights, out_grad, w_gate_up, w_down, second_moment):
    groups = lax.axis_size("narrow")
    wides = lax.axis_size("wide")
    count, width = tokens.shape
    cap = 3 * count // (2 * groups)
    slot = -(-cap // 16) * 16
    chunks = 4
    columns = w_gate_up.shape[2]
    units = w_down.shape[1]
    all_rows = groups * 2 * slot
    late = groups // 2 - 1
    dma = pltpu.SemaphoreType.DMA
    any_spec = pl.BlockSpec(memory_space=pl.ANY)
    vmem_spec = pl.BlockSpec(memory_space=pltpu.VMEM)
    last_rows = late * 2 * slot
    held = pl.pallas_call(
        functools.partial(kernel, groups, wides, cap, slot, chunks),
        out_shape=(
            pltpu.VMEM((width, columns), f32),
            pltpu.VMEM((last_rows, width), bf16),
            pltpu.VMEM((last_rows, columns), bf16),
            pltpu.VMEM((units, width), bf16),
        ),
        in_specs=[vmem_spec, vmem_spec] + [pl.BlockSpec(memory_space=pltpu.HBM)] * 5,
        out_specs=(vmem_spec,) * 4,
        scratch_shapes=[
            pltpu.VMEM((count, width), bf16),
            pltpu.VMEM((count, width), bf16),
            pltpu.VMEM((width, columns), bf16),
            pltpu.VMEM((units, width), bf16),
            pltpu.VMEM((units, width), bf16),
            pltpu.VMEM((groups, slot, width), bf16),
            pltpu.VMEM((groups, slot, width), bf16),
            pltpu.VMEM((all_rows, width), bf16),
            pltpu.VMEM((all_rows, width), bf16),
            pltpu.VMEM((all_rows, columns), bf16),
            pltpu.VMEM((all_rows, units), bf16),
            pltpu.VMEM((units, width), f32),
            dma((5,)),
            dma((groups,)), dma((groups,)), dma((groups,)), dma((groups,)),
            dma((late * chunks,)), dma((late * chunks,)),
            dma((groups,)), dma((groups,)), dma((groups,)), dma((groups,)),
            dma((late * chunks,)), dma((late * chunks,)),
        ],
        compiler_params=pltpu.CompilerParams(
            collective_id=0, has_side_effects=True, vmem_limit_bytes=LIMIT
        ),
    )(
        expert_ids.reshape(1, count), route_weights.reshape(1, count),
        tokens, out_grad, w_gate_up, w_down, second_moment,
    )
    return pl.pallas_call(
        final_kernel,
        out_shape=(
            jax.ShapeDtypeStruct((1, width, columns), bf16),
            jax.ShapeDtypeStruct((1, units, width), bf16),
        ),
        in_specs=[vmem_spec] * 4,
        out_specs=(any_spec, any_spec),
        scratch_shapes=[pltpu.VMEM((width, columns), bf16), dma((width // 256 + 1,))],
        compiler_params=pltpu.CompilerParams(vmem_limit_bytes=LIMIT),
    )(*held)


def solution(mesh):
    placed = (
        P(("wide", "narrow"), None),
        P(("wide", "narrow")),
        P(("wide", "narrow")),
        P(("wide", "narrow"), None),
        P(("wide", "narrow"), None, None),
        P(("wide", "narrow"), None, None),
        P(("wide", "narrow"), None, None),
    )
    return jax.shard_map(
        body,
        mesh=mesh,
        in_specs=placed,
        out_specs=(P(("wide", "narrow"), None, None), P(("wide", "narrow"), None, None)),
        check_vma=False,
    )
```

```python
import functools

import jax
import jax.numpy as jnp
from jax import lax
from jax.experimental import pallas as pl
from jax.experimental.pallas import tpu as pltpu
from jax.sharding import PartitionSpec as P

second_correction = 1.0 - 0.95**10
bf16 = jnp.bfloat16
f32 = jnp.float32
LIMIT = 32 * 1024 * 1024


def mm(a, b, dims):
    return lax.dot_general(a, b, (dims, ((), ())), preferred_element_type=f32)


def kernel(
    groups, wides, cap, slot, chunks,
    ids_hbm, rw_hbm, tok_hbm, og_hbm, wgu_hbm, wdn_hbm, sm_hbm,
    acc_p, rows_last, pre_last, ustage,
    ids, rw, tok, og, wgu, wdn, sm, px, pd, rx, rd, pre, hid, acc_d,
    in_sem, sx, rxs, sd, rds, sc, rcs, fsx, frx, fsd, frd, fsc, frc,
):
    half = groups // 2
    width = tok.shape[1]
    hidden_units = wdn.shape[0]
    wide = lax.axis_index("wide")
    narrow = lax.axis_index("narrow")
    home = narrow // 2
    parity = lax.rem(narrow, 2)
    ahead = lax.rem(wide + 1, wides)
    behind = lax.rem(wide + wides - 1, wides)

    def device(w, n):
        return {"wide": w, "narrow": n}

    def expert_at(j):
        return lax.rem(home + j, half)

    sibling = device(wide, 2 * home + 1 - parity)

    order = [(0, 0), (1, 0)] + [(0, j) for j in range(1, half)] + [(1, j) for j in range(1, half)]
    early = 2 + (half - 1)
    late = half - 1
    remote_early = list(range(1, early))
    late_list = list(range(early, early + late))

    loads = []
    for i, (src, dst) in enumerate(
        (
            (tok_hbm, tok), (og_hbm, og), (wgu_hbm.at[0], wgu), (wdn_hbm.at[0], wdn),
            (sm_hbm.at[0], sm), (ids_hbm, ids), (rw_hbm, rw),
        )
    ):
        copy = pltpu.make_async_copy(src, dst, in_sem.at[i])
        loads.append(copy)
    for i in (5, 0, 6, 1, 2, 3, 4):
        loads[i].start()

    barrier = pltpu.get_barrier_semaphore()
    partners = [device(behind, 2 * expert_at(j) + parity) for j in range(half)]
    partners += [device(wide, 2 * expert_at(j) + parity) for j in range(1, half)]
    partners.append(sibling)
    for partner in partners:
        pl.semaphore_signal(barrier, inc=1, device_id=partner, device_id_type=pl.DeviceIdType.MESH)

    loads[5].wait()
    loads[6].wait()
    count = tok.shape[0]
    labels = ids[...]
    pad_groups = max(8, groups)
    onehot = (lax.broadcasted_iota(jnp.int32, (pad_groups, count), 0) == labels).astype(f32)
    before = (
        lax.broadcasted_iota(jnp.int32, (count, count), 0)
        < lax.broadcasted_iota(jnp.int32, (count, count), 1)
    ).astype(f32)
    counted = mm(onehot.astype(bf16), before.astype(bf16), ((1,), (0,)))
    within = jnp.sum(counted * onehot, axis=0, keepdims=True).astype(jnp.int32)
    weights = rw[...]
    slots = lax.broadcasted_iota(jnp.int32, (slot, count), 0)

    def select_of(b):
        kind, j = order[b]
        value = kind * half + expert_at(j)
        return jnp.logical_and(labels == value, slots == within)

    def rows(b, h):
        return pl.ds((2 * b + h) * slot, slot)

    def dest(b):
        kind, j = order[b]
        return device(ahead if kind else wide, 2 * expert_at(j) + parity)

    def remote(src, dst, s, r, dev):
        return pltpu.make_async_remote_copy(
            src_ref=src, dst_ref=dst, send_sem=s, recv_sem=r,
            device_id=dev, device_id_type=pl.DeviceIdType.MESH,
        )

    part = width // chunks

    def send_x(b):
        return remote(px.at[b], rx.at[rows(b, 0)], sx.at[b], rxs.at[b], dest(b))

    def send_d(b):
        return remote(pd.at[b], rd.at[rows(b, 0)], sd.at[b], rds.at[b], dest(b))

    def send_c(b, c):
        cols = pl.ds(c * part, part)
        i = (b - early) * chunks + c
        return remote(
            pd.at[b, :, cols], rd.at[rows(b, 0), cols], sc.at[i], rcs.at[i], dest(b)
        )

    def forward_x(b):
        return remote(rx.at[rows(b, 0)], rx.at[rows(b, 1)], fsx.at[b], frx.at[b], sibling)

    def forward_d(b):
        return remote(rd.at[rows(b, 0)], rd.at[rows(b, 1)], fsd.at[b], frd.at[b], sibling)

    def forward_c(b, c):
        cols = pl.ds(c * part, part)
        i = (b - early) * chunks + c
        return remote(
            rd.at[rows(b, 0), cols], rd.at[rows(b, 1), cols], fsc.at[i], frc.at[i], sibling
        )

    started = []

    def go(copy):
        copy.start()
        started.append(copy)

    def pack_x(b):
        return mm(select_of(b).astype(f32).astype(bf16), tok[...], ((1,), (0,))).astype(bf16)

    def pack_d(b):
        select = select_of(b)
        weight = jnp.sum(jnp.where(select, weights, 0.0), axis=1, keepdims=True)
        placed = mm(select.astype(f32).astype(bf16), og[...], ((1,), (0,)))
        return (weight * placed).astype(bf16)

    loads[0].wait()
    for b in remote_early:
        px[b] = pack_x(b)
    pl.semaphore_wait(barrier, len(partners))
    for b in remote_early:
        go(send_x(b))
    loads[1].wait()
    for b in remote_early:
        pd[b] = pack_d(b)
    for b in late_list:
        px[b] = pack_x(b)
    for b in remote_early:
        go(send_d(b))
    for b in late_list:
        go(send_x(b))
    for b in late_list:
        pd[b] = pack_d(b)
    rx[rows(0, 0), :] = pack_x(0)
    for b in late_list:
        for c in range(chunks):
            go(send_c(b, c))
    rd[rows(0, 0), :] = pack_d(0)
    go(forward_x(0))
    go(forward_d(0))
    loads[2].wait()
    loads[3].wait()

    def project(r):
        projected = mm(rx[r, :], wgu[...], ((1,), (0,)))
        gate_pre = projected[:, :hidden_units]
        up_pre = projected[:, hidden_units:]
        logistic = jax.nn.sigmoid(gate_pre)
        swished = gate_pre * logistic
        hid[r, :] = (swished * up_pre).astype(bf16)
        return up_pre * logistic * (1.0 + gate_pre * (1.0 - logistic)), swished

    def finish(target, r, hidden_grad, factors):
        target[r, :] = jnp.concatenate(
            [hidden_grad * factors[0], hidden_grad * factors[1]], axis=1
        ).astype(bf16)

    for b in remote_early:
        send_x(b).wait_recv()
        go(forward_x(b))
    for b in remote_early:
        send_d(b).wait_recv()
        go(forward_d(b))
    for b in range(early):
        forward_x(b).wait_recv()
        forward_d(b).wait_recv()
    first = pl.ds(0, early * 2 * slot)
    finish(pre, first, mm(rd[first, :], wdn[...], ((1,), (1,))), project(first))
    for i in range(width // 256):
        cols = pl.ds(i * 256, 256)
        acc_p[cols, :] = mm(rx[first, cols], pre[first, :], ((0,), (0,)))
        acc_d[:, cols] = mm(hid[first, :], rd[first, cols], ((0,), (0,)))

    for b in late_list:
        send_x(b).wait_recv()
        go(forward_x(b))
    for b in late_list:
        forward_x(b).wait_recv()
    last = pl.ds(early * 2 * slot, late * 2 * slot)
    factors = project(last)
    rows_last[...] = rx[last, :]
    loads[4].wait()
    hidden_grad = jnp.zeros((late * 2 * slot, hidden_units), f32)

    def relay(c):
        for b in late_list:
            send_c(b, c).wait_recv()
            go(forward_c(b, c))

    relay(0)
    for c in range(chunks):
        if c + 1 < chunks:
            relay(c + 1)
        for b in late_list:
            forward_c(b, c).wait_recv()
        cols = pl.ds(c * part, part)
        hidden_grad = hidden_grad + mm(rd[last, cols], wdn[:, cols], ((1,), (1,)))
        total = acc_d[:, cols] + mm(hid[last, :], rd[last, cols], ((0,), (0,)))
        second = 0.95 * sm[:, cols].astype(f32) + 0.05 * total * total
        update = total / (jnp.sqrt(second / second_correction) + 1e-08)
        ustage[:, cols] = (update + 0.1 * wdn[:, cols].astype(f32)).astype(bf16)

    finish(pre_last, slice(None), hidden_grad, factors)
    for copy in started:
        copy.wait_send()


def final_kernel(acc_p, rows_last, pre_last, update, gout, uout, gstage, out_sem):
    tiles = acc_p.shape[0] // 256
    outs = [pltpu.make_async_copy(update, uout.at[0], out_sem.at[tiles])]
    outs[0].start()
    for i in range(tiles):
        r = pl.ds(i * 256, 256)
        gstage[r, :] = (acc_p[r, :] + mm(rows_last[:, r], pre_last[...], ((0,), (0,)))).astype(bf16)
        copy = pltpu.make_async_copy(gstage.at[r], gout.at[0, r], out_sem.at[i])
        copy.start()
        outs.append(copy)
    for copy in outs:
        copy.wait()


def body(tokens, expert_ids, route_weights, out_grad, w_gate_up, w_down, second_moment):
    groups = lax.axis_size("narrow")
    wides = lax.axis_size("wide")
    count, width = tokens.shape
    cap = 3 * count // (2 * groups)
    slot = -(-cap // 16) * 16
    chunks = 4
    columns = w_gate_up.shape[2]
    units = w_down.shape[1]
    all_rows = groups * 2 * slot
    late = groups // 2 - 1
    dma = pltpu.SemaphoreType.DMA
    any_spec = pl.BlockSpec(memory_space=pl.ANY)
    vmem_spec = pl.BlockSpec(memory_space=pltpu.VMEM)
    last_rows = late * 2 * slot
    held = pl.pallas_call(
        functools.partial(kernel, groups, wides, cap, slot, chunks),
        out_shape=(
            pltpu.VMEM((width, columns), f32),
            pltpu.VMEM((last_rows, width), bf16),
            pltpu.VMEM((last_rows, columns), bf16),
            pltpu.VMEM((units, width), bf16),
        ),
        in_specs=[any_spec] * 7,
        out_specs=(vmem_spec,) * 4,
        scratch_shapes=[
            pltpu.VMEM((1, count), jnp.int32),
            pltpu.VMEM((1, count), f32),
            pltpu.VMEM((count, width), bf16),
            pltpu.VMEM((count, width), bf16),
            pltpu.VMEM((width, columns), bf16),
            pltpu.VMEM((units, width), bf16),
            pltpu.VMEM((units, width), bf16),
            pltpu.VMEM((groups, slot, width), bf16),
            pltpu.VMEM((groups, slot, width), bf16),
            pltpu.VMEM((all_rows, width), bf16),
            pltpu.VMEM((all_rows, width), bf16),
            pltpu.VMEM((all_rows, columns), bf16),
            pltpu.VMEM((all_rows, units), bf16),
            pltpu.VMEM((units, width), f32),
            dma((7,)),
            dma((groups,)), dma((groups,)), dma((groups,)), dma((groups,)),
            dma((late * chunks,)), dma((late * chunks,)),
            dma((groups,)), dma((groups,)), dma((groups,)), dma((groups,)),
            dma((late * chunks,)), dma((late * chunks,)),
        ],
        compiler_params=pltpu.CompilerParams(
            collective_id=0, has_side_effects=True, vmem_limit_bytes=LIMIT
        ),
    )(
        *(
            pltpu.with_memory_space_constraint(value, pltpu.HBM)
            for value in (
                expert_ids.reshape(1, count), route_weights.reshape(1, count),
                tokens, out_grad, w_gate_up, w_down, second_moment,
            )
        ),
    )
    return pl.pallas_call(
        final_kernel,
        out_shape=(
            jax.ShapeDtypeStruct((1, width, columns), bf16),
            jax.ShapeDtypeStruct((1, units, width), bf16),
        ),
        in_specs=[vmem_spec] * 4,
        out_specs=(any_spec, any_spec),
        scratch_shapes=[pltpu.VMEM((width, columns), bf16), dma((width // 256 + 1,))],
        compiler_params=pltpu.CompilerParams(vmem_limit_bytes=LIMIT),
    )(*held)


def solution(mesh):
    placed = (
        P(("wide", "narrow"), None),
        P(("wide", "narrow")),
        P(("wide", "narrow")),
        P(("wide", "narrow"), None),
        P(("wide", "narrow"), None, None),
        P(("wide", "narrow"), None, None),
        P(("wide", "narrow"), None, None),
    )
    return jax.shard_map(
        body,
        mesh=mesh,
        in_specs=placed,
        out_specs=(P(("wide", "narrow"), None, None), P(("wide", "narrow"), None, None)),
        check_vma=False,
    )
```

```python
import functools

import jax
import jax.numpy as jnp
from jax import lax
from jax.experimental import pallas as pl
from jax.experimental.pallas import tpu as pltpu
from jax.sharding import PartitionSpec as P

second_correction = 1.0 - 0.95**10
bf16 = jnp.bfloat16
f32 = jnp.float32
LIMIT = 32 * 1024 * 1024


def mm(a, b, dims):
    return lax.dot_general(a, b, (dims, ((), ())), preferred_element_type=f32)


def kernel(
    groups, wides, cap, slot, chunks,
    ids_hbm, rw_hbm, tok_hbm, og_hbm, wgu_hbm, wdn_hbm, sm_hbm,
    acc_p, rows_last, pre_last, ustage,
    ids, rw, tok, og, wgu, wdn, sm, px, pd, rx, rd, pre, hid, acc_d,
    in_sem, sx, rxs, sd, rds, sc, rcs, fsx, frx, fsd, frd, fsc, frc,
):
    half = groups // 2
    width = tok.shape[1]
    hidden_units = wdn.shape[0]
    wide = lax.axis_index("wide")
    narrow = lax.axis_index("narrow")
    home = narrow // 2
    parity = lax.rem(narrow, 2)
    ahead = lax.rem(wide + 1, wides)
    behind = lax.rem(wide + wides - 1, wides)

    def device(w, n):
        return {"wide": w, "narrow": n}

    def expert_at(j):
        return lax.rem(home + j, half)

    sibling = device(wide, 2 * home + 1 - parity)

    order = [(0, 0), (1, 0)] + [(0, j) for j in range(1, half)] + [(1, j) for j in range(1, half)]
    early = 2 + (half - 1)
    late = half - 1
    remote_early = list(range(2, early)) + [1]
    late_list = list(range(early, early + late))

    loads = []
    for i, (src, dst) in enumerate(
        (
            (tok_hbm, tok), (og_hbm, og), (wgu_hbm.at[0], wgu), (wdn_hbm.at[0], wdn),
            (sm_hbm.at[0], sm), (ids_hbm, ids), (rw_hbm, rw),
        )
    ):
        copy = pltpu.make_async_copy(src, dst, in_sem.at[i])
        loads.append(copy)
    for i in (5, 0, 6, 1, 2, 3, 4):
        loads[i].start()

    barrier = pltpu.get_barrier_semaphore()
    partners = [device(behind, 2 * expert_at(j) + parity) for j in range(half)]
    partners += [device(wide, 2 * expert_at(j) + parity) for j in range(1, half)]
    partners.append(sibling)
    for partner in partners:
        pl.semaphore_signal(barrier, inc=1, device_id=partner, device_id_type=pl.DeviceIdType.MESH)

    loads[5].wait()
    loads[6].wait()
    count = tok.shape[0]
    labels = ids[...]
    pad_groups = max(8, groups)
    onehot = (lax.broadcasted_iota(jnp.int32, (pad_groups, count), 0) == labels).astype(f32)
    before = (
        lax.broadcasted_iota(jnp.int32, (count, count), 0)
        < lax.broadcasted_iota(jnp.int32, (count, count), 1)
    ).astype(f32)
    counted = mm(onehot.astype(bf16), before.astype(bf16), ((1,), (0,)))
    within = jnp.sum(counted * onehot, axis=0, keepdims=True).astype(jnp.int32)
    weights = rw[...]
    slots = lax.broadcasted_iota(jnp.int32, (slot, count), 0)

    def select_of(b):
        kind, j = order[b]
        value = kind * half + expert_at(j)
        return jnp.logical_and(labels == value, slots == within)

    def rows(b, h):
        return pl.ds((2 * b + h) * slot, slot)

    def dest(b):
        kind, j = order[b]
        return device(ahead if kind else wide, 2 * expert_at(j) + parity)

    def remote(src, dst, s, r, dev):
        return pltpu.make_async_remote_copy(
            src_ref=src, dst_ref=dst, send_sem=s, recv_sem=r,
            device_id=dev, device_id_type=pl.DeviceIdType.MESH,
        )

    part = width // chunks

    def send_x(b):
        return remote(px.at[b], rx.at[rows(b, 0)], sx.at[b], rxs.at[b], dest(b))

    def send_d(b):
        return remote(pd.at[b], rd.at[rows(b, 0)], sd.at[b], rds.at[b], dest(b))

    def send_c(b, c):
        cols = pl.ds(c * part, part)
        i = (b - early) * chunks + c
        return remote(
            pd.at[b, :, cols], rd.at[rows(b, 0), cols], sc.at[i], rcs.at[i], dest(b)
        )

    def forward_x(b):
        return remote(rx.at[rows(b, 0)], rx.at[rows(b, 1)], fsx.at[b], frx.at[b], sibling)

    def forward_d(b):
        return remote(rd.at[rows(b, 0)], rd.at[rows(b, 1)], fsd.at[b], frd.at[b], sibling)

    def forward_c(b, c):
        cols = pl.ds(c * part, part)
        i = (b - early) * chunks + c
        return remote(
            rd.at[rows(b, 0), cols], rd.at[rows(b, 1), cols], fsc.at[i], frc.at[i], sibling
        )

    started = []

    def go(copy):
        copy.start()
        started.append(copy)

    def pack_x(b):
        return mm(select_of(b).astype(f32).astype(bf16), tok[...], ((1,), (0,))).astype(bf16)

    def pack_d(b):
        select = select_of(b)
        weight = jnp.sum(jnp.where(select, weights, 0.0), axis=1, keepdims=True)
        placed = mm(select.astype(f32).astype(bf16), og[...], ((1,), (0,)))
        return (weight * placed).astype(bf16)

    loads[0].wait()
    for b in remote_early:
        px[b] = pack_x(b)
    pl.semaphore_wait(barrier, len(partners))
    for b in remote_early:
        go(send_x(b))
    loads[1].wait()
    for b in remote_early:
        pd[b] = pack_d(b)
    for b in late_list:
        px[b] = pack_x(b)
    for b in remote_early:
        go(send_d(b))
    for b in late_list:
        go(send_x(b))
    for b in late_list:
        pd[b] = pack_d(b)
    rx[rows(0, 0), :] = pack_x(0)
    for b in late_list:
        for c in range(chunks):
            go(send_c(b, c))
    rd[rows(0, 0), :] = pack_d(0)
    go(forward_x(0))
    go(forward_d(0))
    loads[2].wait()
    loads[3].wait()

    def project(r):
        projected = mm(rx[r, :], wgu[...], ((1,), (0,)))
        gate_pre = projected[:, :hidden_units]
        up_pre = projected[:, hidden_units:]
        logistic = jax.nn.sigmoid(gate_pre)
        swished = gate_pre * logistic
        hid[r, :] = (swished * up_pre).astype(bf16)
        return up_pre * logistic * (1.0 + gate_pre * (1.0 - logistic)), swished

    def finish(target, r, hidden_grad, factors):
        target[r, :] = jnp.concatenate(
            [hidden_grad * factors[0], hidden_grad * factors[1]], axis=1
        ).astype(bf16)

    for b in remote_early:
        send_x(b).wait_recv()
        go(forward_x(b))
    for b in remote_early:
        send_d(b).wait_recv()
        go(forward_d(b))
    for b in range(early):
        forward_x(b).wait_recv()
        forward_d(b).wait_recv()
    first = pl.ds(0, early * 2 * slot)
    finish(pre, first, mm(rd[first, :], wdn[...], ((1,), (1,))), project(first))
    for i in range(width // 256):
        cols = pl.ds(i * 256, 256)
        acc_p[cols, :] = mm(rx[first, cols], pre[first, :], ((0,), (0,)))
        acc_d[:, cols] = mm(hid[first, :], rd[first, cols], ((0,), (0,)))

    for b in late_list:
        send_x(b).wait_recv()
        go(forward_x(b))
    for b in late_list:
        forward_x(b).wait_recv()
    last = pl.ds(early * 2 * slot, late * 2 * slot)
    factors = project(last)
    rows_last[...] = rx[last, :]
    loads[4].wait()
    hidden_grad = jnp.zeros((late * 2 * slot, hidden_units), f32)

    def relay(c):
        for b in late_list:
            send_c(b, c).wait_recv()
            go(forward_c(b, c))

    relay(0)
    for c in range(chunks):
        if c + 1 < chunks:
            relay(c + 1)
        for b in late_list:
            forward_c(b, c).wait_recv()
        cols = pl.ds(c * part, part)
        hidden_grad = hidden_grad + mm(rd[last, cols], wdn[:, cols], ((1,), (1,)))
        total = acc_d[:, cols] + mm(hid[last, :], rd[last, cols], ((0,), (0,)))
        second = 0.95 * sm[:, cols].astype(f32) + 0.05 * total * total
        update = total / (jnp.sqrt(second / second_correction) + 1e-08)
        ustage[:, cols] = (update + 0.1 * wdn[:, cols].astype(f32)).astype(bf16)

    finish(pre_last, slice(None), hidden_grad, factors)
    for copy in started:
        copy.wait_send()


def final_kernel(acc_p, rows_last, pre_last, update, gout, uout, gstage, out_sem):
    tiles = acc_p.shape[0] // 256
    outs = [pltpu.make_async_copy(update, uout.at[0], out_sem.at[tiles])]
    outs[0].start()
    for i in range(tiles):
        r = pl.ds(i * 256, 256)
        gstage[r, :] = (acc_p[r, :] + mm(rows_last[:, r], pre_last[...], ((0,), (0,)))).astype(bf16)
        copy = pltpu.make_async_copy(gstage.at[r], gout.at[0, r], out_sem.at[i])
        copy.start()
        outs.append(copy)
    for copy in outs:
        copy.wait()


def body(tokens, expert_ids, route_weights, out_grad, w_gate_up, w_down, second_moment):
    groups = lax.axis_size("narrow")
    wides = lax.axis_size("wide")
    count, width = tokens.shape
    cap = 3 * count // (2 * groups)
    slot = -(-cap // 16) * 16
    chunks = 4
    columns = w_gate_up.shape[2]
    units = w_down.shape[1]
    all_rows = groups * 2 * slot
    late = groups // 2 - 1
    dma = pltpu.SemaphoreType.DMA
    any_spec = pl.BlockSpec(memory_space=pl.ANY)
    vmem_spec = pl.BlockSpec(memory_space=pltpu.VMEM)
    last_rows = late * 2 * slot
    held = pl.pallas_call(
        functools.partial(kernel, groups, wides, cap, slot, chunks),
        out_shape=(
            pltpu.VMEM((width, columns), f32),
            pltpu.VMEM((last_rows, width), bf16),
            pltpu.VMEM((last_rows, columns), bf16),
            pltpu.VMEM((units, width), bf16),
        ),
        in_specs=[any_spec] * 7,
        out_specs=(vmem_spec,) * 4,
        scratch_shapes=[
            pltpu.VMEM((1, count), jnp.int32),
            pltpu.VMEM((1, count), f32),
            pltpu.VMEM((count, width), bf16),
            pltpu.VMEM((count, width), bf16),
            pltpu.VMEM((width, columns), bf16),
            pltpu.VMEM((units, width), bf16),
            pltpu.VMEM((units, width), bf16),
            pltpu.VMEM((groups, slot, width), bf16),
            pltpu.VMEM((groups, slot, width), bf16),
            pltpu.VMEM((all_rows, width), bf16),
            pltpu.VMEM((all_rows, width), bf16),
            pltpu.VMEM((all_rows, columns), bf16),
            pltpu.VMEM((all_rows, units), bf16),
            pltpu.VMEM((units, width), f32),
            dma((7,)),
            dma((groups,)), dma((groups,)), dma((groups,)), dma((groups,)),
            dma((late * chunks,)), dma((late * chunks,)),
            dma((groups,)), dma((groups,)), dma((groups,)), dma((groups,)),
            dma((late * chunks,)), dma((late * chunks,)),
        ],
        compiler_params=pltpu.CompilerParams(
            collective_id=0, has_side_effects=True, vmem_limit_bytes=LIMIT
        ),
    )(
        *(
            pltpu.with_memory_space_constraint(value, pltpu.HBM)
            for value in (
                expert_ids.reshape(1, count), route_weights.reshape(1, count),
                tokens, out_grad, w_gate_up, w_down, second_moment,
            )
        ),
    )
    return pl.pallas_call(
        final_kernel,
        out_shape=(
            jax.ShapeDtypeStruct((1, width, columns), bf16),
            jax.ShapeDtypeStruct((1, units, width), bf16),
        ),
        in_specs=[vmem_spec] * 4,
        out_specs=(any_spec, any_spec),
        scratch_shapes=[pltpu.VMEM((width, columns), bf16), dma((width // 256 + 1,))],
        compiler_params=pltpu.CompilerParams(vmem_limit_bytes=LIMIT),
    )(*held)


def solution(mesh):
    placed = (
        P(("wide", "narrow"), None),
        P(("wide", "narrow")),
        P(("wide", "narrow")),
        P(("wide", "narrow"), None),
        P(("wide", "narrow"), None, None),
        P(("wide", "narrow"), None, None),
        P(("wide", "narrow"), None, None),
    )
    return jax.shard_map(
        body,
        mesh=mesh,
        in_specs=placed,
        out_specs=(P(("wide", "narrow"), None, None), P(("wide", "narrow"), None, None)),
        check_vma=False,
    )
```
